256 devices in a mesh: row: 32 (over x, z), col: 8 (over y, core).
Axes of the slice: x: 4, y: 4, z: 8, core: 2. Of those that a mesh axis runs over, the one named last changes fastest.
Arguments:
- matrix: float32 [2, 32, 256, 8, 8, 256], P(None, 'row', None, None, 'col'), may hold values from -160 to 8000, as said below
Outputs:
- trailing: float32 [2, 32, 256, 8, 8, 256], P(None, 'row', None, None, 'col')
- factor_panels: float32 [2, 32, 256, 768], P(None, 'row')
The draws below stay inside these ranges and needn't reach their ends.
Inputs may be any that keep to these rules, and one draw needn't show every extreme that they name: matrix is symmetric positive definite with condition number at most about 2,000.
All inputs are finite; a program needn't handle non-finite values.
Results may differ from the reference program's by a relative error of at most 0.00018.
Values sent between devices are 32-bit elements; how exact they have to be, the bound alone decides.
A program may use at most 64 MiB of HBM per device.

```python
import jax
import jax.numpy as jnp
from jax import lax

TILE = 256
TILE_ROWS = 2
PANELS = 3
TILE_COLS = 8
N_ROW = 32
N_COL = 8


def draw_matrix(key, part):
    order = TILE_ROWS * N_ROW * TILE
    key_base, key_diag = jax.random.split(key, 2)
    base = jnp.clip(jax.random.normal(key_base, (order, order), jnp.float32), -6.0, 6.0)
    sym = (base + base.T) * 0.70710677
    extra = 2.6 * jnp.sqrt(jnp.float32(order)) * (1.0 + 0.3 * jax.random.uniform(key_diag, (order,), jnp.float32))
    index = jnp.arange(order)
    sym = sym.at[index, index].add(extra)
    sym = sym + 1.5 * jnp.ones((order, order), jnp.float32)
    return sym.reshape(TILE_ROWS, N_ROW, TILE, TILE_COLS, N_COL, TILE)


def setup_inputs(seed: int = 0) -> dict:
    key_list = jax.random.split(jax.random.key(seed), 2)
    return {
        "matrix": draw_matrix(jax.random.fold_in(key_list[1], 71), 0),
    }


def reference(matrix):
    order = TILE_ROWS * N_ROW * TILE
    work = matrix.reshape(order, order)
    row_numbers = jnp.arange(order)
    collected = []
    for step in range(PANELS):
        start = step * TILE
        column = work[:, start:start + TILE]
        lower = jnp.linalg.cholesky(column[start:start + TILE])
        inverse = jax.scipy.linalg.solve_triangular(lower, jnp.eye(TILE, dtype=work.dtype), lower=True)
        panel = jnp.dot(column, inverse.T, precision=lax.Precision.HIGHEST)
        panel = jnp.where((row_numbers >= start)[:, None], panel, jnp.zeros_like(panel))
        work = work - jnp.dot(panel, panel.T, precision=lax.Precision.HIGHEST)
        collected.append(panel)
    factor_panels = jnp.concatenate(collected, axis=1).reshape(TILE_ROWS, N_ROW, TILE, PANELS * TILE)
    return (work.reshape(matrix.shape), factor_panels)
```

```python
import jax
import jax.numpy as jnp
from jax import lax
from jax.experimental import pallas as pl
from jax.experimental.pallas import tpu as pltpu
from jax.sharding import PartitionSpec as P

PANELS = 3
HI = lax.Precision.HIGHEST
N=768; NB=128

def dotg(a,b,ca,cb,prec=HI):
    return lax.dot_general(a,b,(((ca,),(cb,)),((),())),precision=prec,preferred_element_type=jnp.float32)


def factor128(load, store_l):
    sub = lax.broadcasted_iota(jnp.int32,(8,128),0)
    lane = lax.broadcasted_iota(jnp.int32,(8,128),1)
    full=(8,128)
    bc=lambda v: jnp.broadcast_to(v,full)
    S=[load(g) for g in range(16)]
    X=[jnp.where(lane==sub+8*g,1.0,0.0).astype(jnp.float32) for g in range(16)]
    for g in range(16):
        V=S[g]; XV=X[g]
        col=[bc(V[:,8*g+j:8*g+j+1]) for j in range(8)]
        a={(i,j):bc(col[j][i:i+1,:]) for j in range(8) for i in range(j,8)}
        y=[bc(V[i:i+1,:]) for i in range(8)]
        w=[bc(XV[i:i+1,:]) for i in range(8)]
        r=[None]*8; m={}
        XI=jnp.zeros(full,jnp.float32)
        for j in range(8):
            rs=lax.rsqrt(a[j,j]); r[j]=rs*rs
            XI=jnp.where(sub==j,w[j]*rs,XI)
            for i in range(j+1,8):
                m[i,j]=a[i,j]*r[j]
            for k in range(j+1,8):
                for i in range(k,8):
                    a[i,k]=a[i,k]-m[i,j]*a[k,j]
            for i in range(j+1,8):
                y[i]=y[i]-m[i,j]*y[j]
                w[i]=w[i]-m[i,j]*w[j]
        store_l(g,XI)
        if g<15:
            z=[None]*8; zx=[None]*8
            for j in range(7,-1,-1):
                z[j]=y[j]*r[j]; zx[j]=w[j]*r[j]
                for k in range(7,j,-1):
                    z[j]=z[j]-m[k,j]*z[k]; zx[j]=zx[j]-m[k,j]*zx[k]
            for h in range(g+1,16):
                s=S[h]; x=X[h]
                cb=[bc(s[:,8*g+j:8*g+j+1]) for j in range(8)]
                t=[cb[j]*z[j] for j in range(8)]
                tx=[cb[j]*zx[j] for j in range(8)]
                tree=lambda t:((t[0]+t[1])+(t[2]+t[3]))+((t[4]+t[5])+(t[6]+t[7]))
                S[h]=s-tree(t); X[h]=x-tree(tx)

def kern(c_ref, u_ref, x_ref, linv):
    r0=lax.broadcasted_iota(jnp.int32,(N,N),0); c0=lax.broadcasted_iota(jnp.int32,(N,N),1)
    u_ref[...]=c_ref[...]
    x_ref[...]=jnp.where(r0==c0,1.0,0.0).astype(jnp.float32)
    def step(t,_):
        o=pl.multiple_of(t*NB,NB)
        def load(g): return u_ref[pl.ds(pl.multiple_of(o+8*g,8),8), pl.ds(o,NB)]
        def store(g,v): linv[8*g:8*g+8,:]=v
        factor128(load,store)
        li=linv[...]
        ur=dotg(li,u_ref[pl.ds(o,NB),:],1,0)
        xr=dotg(li,x_ref[pl.ds(o,NB),:],1,0)
        u_ref[pl.ds(o,NB),:]=ur
        x_ref[pl.ds(o,NB),:]=xr
        for b in range(1,6):
            @pl.when(b>t)
            def _():
                ub=u_ref[pl.ds(o,NB), b*NB:(b+1)*NB]
                u_ref[b*NB:(b+1)*NB,:]-=dotg(ub,ur,0,0)
                x_ref[b*NB:(b+1)*NB,:]-=dotg(ub,xr,0,0)
        return 0
    lax.fori_loop(0,6,step,0)

def chol(c):
    return pl.pallas_call(kern,out_shape=(jax.ShapeDtypeStruct((N,N),jnp.float32),)*2,
      in_specs=[pl.BlockSpec(memory_space=pltpu.VMEM)],
      out_specs=(pl.BlockSpec(memory_space=pltpu.VMEM),)*2,
      scratch_shapes=[pltpu.VMEM((NB,NB),jnp.float32)],
      compiler_params=pltpu.CompilerParams(vmem_limit_bytes=48<<20))(c)
MESH = pl.DeviceIdType.MESH
CORNER = ((0, 0), (1, 0), (1, 1), (2, 0), (2, 1), (2, 2))
PIECES = 48


def comm_kernel(a0, A, B, C, asend, arecv, ysend, crecv, csend, psend, precv, brecv, bsend, loc):
    p = lax.axis_index("row")
    q = lax.axis_index("col")
    x = p // 8
    z = p % 8
    core = q % 2
    partner = q + 1 - 2 * core

    def at(px, pz):
        return (lax.rem(px + 4, 4) * 8 + lax.rem(pz + 8, 8), q)

    def along(d):
        return (p, lax.rem(q + d, 8))

    def rcopy(src, dst, ss, rs, dev):
        return pltpu.make_async_remote_copy(
            src_ref=src, dst_ref=dst, send_sem=ss, recv_sem=rs, device_id=dev, device_id_type=MESH
        )

    def arrived(ref, sem):
        pltpu.make_async_copy(ref, ref, sem).wait()

    barrier = pltpu.get_barrier_semaphore()
    for d in range(1, 8):
        pl.semaphore_signal(barrier, inc=1, device_id=along(d), device_id_type=MESH)
    for dx, dz in ((1, 0), (-1, 0), (0, 1), (0, -1)):
        pl.semaphore_signal(barrier, inc=1, device_id=at(x + dx, z + dz), device_id_type=MESH)
    pl.semaphore_wait(barrier, 11)

    def quarter(c, u):
        return pl.ds(pl.multiple_of((c + 2 * u) * 64, 64), 64)

    def ycopy(idx, d, u):
        rows = quarter(lax.rem(q + d, 2), u)
        return rcopy(a0.at[0, rows, :], C.at[idx, rows, :], ysend.at[(d - 1) * 2 + u], crecv.at[idx, u], along(d))

    for idx, (i, j) in enumerate(CORNER):

        @pl.when((p == i) & (q == j))
        def _(idx=idx):
            pltpu.make_async_copy(a0.at[0], C.at[idx], loc.at[2]).start()
            for u in range(2):
                for d in range(1, 8):
                    ycopy(idx, d, u).start()
            pltpu.make_async_copy(a0.at[0], C.at[idx], loc.at[2]).wait()

    first = lax.rem(z - q + 8, 8)

    def acopy(k, a, d):
        return rcopy(a0.at[a], A.at[k, a], asend.at[a, d - 1], arecv.at[k, a], along(d))

    for k in range(3):

        @pl.when(q == k)
        def _(k=k):
            for a in range(2):
                pltpu.make_async_copy(a0.at[a], A.at[k, a], loc.at[a]).start()
            for now in (True, False):
                for a in range(2):
                    for d in range(1, 8):

                        @pl.when((d == first) if now else (d != first))
                        def _(a=a, d=d):
                            acopy(k, a, d).start()

    def hops(x0, z0, typ, sx, sz):
        dx = lax.rem(x - x0 + 4, 4)
        dz = lax.rem(sz * (z - z0) + 16, 8)
        cz = (typ == 1) | (dx == 0)
        cx = (typ == 0) | (dz == 0)
        return (
            ((x, z + sz), cz & (dz <= 3)),
            ((x, z - sz), cz & ((dz == 0) | (dz >= 6))),
            ((x + 1, z), cx & ((dx == 0) | ((dx == 1) & (sx == 1)))),
            ((x - 1, z), cx & ((dx == 0) | ((dx == 3) & (sx == 0)))),
        )

    def corner(e, end):
        idx, u = e // 2, e % 2
        i, j = CORNER[idx]
        ref = C.at[idx, quarter(core, u), :]
        other = C.at[idx, quarter(1 - core, u), :]
        mine = (p == i) & (q == j)
        its = (p == i) & (partner == j)
        if not end:

            @pl.when(jnp.logical_not(mine))
            def _():
                arrived(ref, crecv.at[idx, u])

        for n, (dev, cond) in enumerate(hops(0, i, u, idx % 2, 1)):

            @pl.when(cond)
            def _(n=n, dev=dev):
                c = rcopy(ref, ref, csend.at[e, n], crecv.at[idx, u], at(*dev))
                c.wait_send() if end else c.start()

        @pl.when(jnp.logical_not(its))
        def _():
            c = rcopy(ref, ref, psend.at[e], precv.at[e], (p, partner))
            c.wait_send() if end else c.start()

        if end:

            @pl.when(jnp.logical_not(mine))
            def _():
                arrived(other, precv.at[e])

    def piece(e, end):
        x0 = e % 4
        r = e // 4
        h = r % 2
        a = (r // 2) % 2
        k = r // 4
        typ = jnp.where((r * 2) % 5 < 2, 1, 0)
        root = (x0 == x) & (z == q)
        ref = B.at[x0, a, k, pl.ds(pl.multiple_of(h * 128, 128), 128), :]
        if not end:

            @pl.when(root & (h == 0))
            def _():
                @pl.when(q == k)
                def _():
                    arrived(A.at[k, a], loc.at[a])

                @pl.when(q != k)
                def _():
                    arrived(A.at[k, a], arecv.at[k, a])

                c = pltpu.make_async_copy(A.at[k, a], B.at[x0, a, k], loc.at[3])
                c.start()
                c.wait()

            @pl.when(jnp.logical_not(root))
            def _():
                arrived(ref, brecv.at[e])

        for n, (dev, cond) in enumerate(hops(x0, q, typ, r % 2, 1 - 2 * ((r // 2) % 2))):

            @pl.when(cond)
            def _(n=n, dev=dev):
                c = rcopy(ref, ref, bsend.at[e, n], brecv.at[e], at(*dev))
                c.wait_send() if end else c.start()

    for e in range(12):
        corner(e, False)

    def go(e, _):
        piece(e, False)
        return 0

    lax.fori_loop(0, PIECES, go, 0)

    for k in range(3):
        for a in range(2):

            @pl.when((z != q) & (q == k))
            def _(k=k, a=a):
                arrived(A.at[k, a], loc.at[a])

            @pl.when((z != q) & (q != k))
            def _(k=k, a=a):
                arrived(A.at[k, a], arecv.at[k, a])

    for e in range(12):
        corner(e, True)

    def done(e, _):
        piece(e, True)
        return 0

    lax.fori_loop(0, PIECES, done, 0)

    for idx, (i, j) in enumerate(CORNER):

        @pl.when((p == i) & (q == j))
        def _(idx=idx):
            for d in range(1, 8):
                for u in range(2):
                    ycopy(idx, d, u).wait_send()

    for k in range(3):

        @pl.when(q == k)
        def _(k=k):
            for a in range(2):
                for d in range(1, 8):
                    acopy(k, a, d).wait_send()


def gather(a0):
    f32 = jnp.float32
    dma = pltpu.SemaphoreType.DMA
    return pl.pallas_call(
        comm_kernel,
        out_shape=(
            jax.ShapeDtypeStruct((3, 2, 256, 256), f32),
            jax.ShapeDtypeStruct((4, 2, 3, 256, 256), f32),
            jax.ShapeDtypeStruct((6, 256, 256), f32),
        ),
        in_specs=[pl.BlockSpec(memory_space=pltpu.VMEM)],
        out_specs=(pl.BlockSpec(memory_space=pltpu.VMEM),) * 3,
        scratch_shapes=[
            dma((2, 7)), dma((3, 2)), dma((14,)), dma((6, 2)), dma((12, 4)), dma((12,)), dma((12,)),
            dma((PIECES,)), dma((PIECES, 4)), dma((4,)),
        ],
        compiler_params=pltpu.CompilerParams(collective_id=0, has_side_effects=True, vmem_limit_bytes=40 << 20),
    )(a0)


def body(matrix):
    my_row = lax.axis_index("row")
    tile = matrix.shape[2]
    work = matrix.reshape(2, tile, 8, tile)
    A, B, C = gather(work[:, :, 0, :])
    t = lambda v: v.T
    corner = jnp.block([[C[0], t(C[1]), t(C[3])], [C[1], C[2], t(C[4])], [C[3], C[4], C[5]]])
    _, inv = chol(corner)
    inv = inv.reshape(3, 256, 3, 256)
    row_tiles = jnp.arange(2) * 32 + my_row
    panel = jnp.einsum("maik,njmk->ainj", A, inv, precision=HI)
    panel = jnp.where((row_tiles[:, None] >= jnp.arange(3))[:, None, :, None], panel, 0.0)
    turns = jnp.arange(4) * 8 + lax.axis_index("col")
    tiles = jnp.arange(2)[:, None] * 32 + turns
    mirrored = jnp.einsum("tamik,njmk->atinj", B, inv, precision=HI)
    mirrored = jnp.where((tiles[:, :, None] >= jnp.arange(3))[:, :, None, :, None], mirrored, 0.0)
    mirrored = mirrored.reshape(8, 256, 3, 256)
    work = work - jnp.einsum("ainj,clnj->aicl", panel, mirrored, precision=HI)
    return (work.reshape(matrix.shape), panel.reshape(2, 1, tile, PANELS * tile))


def solution(mesh):
    in_specs = (P(None, "row", None, None, "col", None),)
    out_specs = (P(None, "row", None, None, "col", None), P(None, "row", None, None))
    return jax.shard_map(body, mesh=mesh, in_specs=in_specs, out_specs=out_specs, check_vma=False)
```

```python
import jax
import jax.numpy as jnp
from jax import lax
from jax.experimental import pallas as pl
from jax.experimental.pallas import tpu as pltpu
from jax.sharding import PartitionSpec as P

HI = lax.Precision.HIGHEST


def dots(a, b, dim, precision=HI):
    return lax.dot_general(a, b, (((1,), (dim,)), ((), ())), precision=precision, preferred_element_type=jnp.float32)


def tdot(a, b):
    return dots(a, b, 1)


def ndot(a, b):
    return dots(a, b, 0)


def factor128(load, store_l, poll):
    sub = lax.broadcasted_iota(jnp.int32,(8,128),0)
    lane = lax.broadcasted_iota(jnp.int32,(8,128),1)
    full=(8,128)
    bc=lambda v: jnp.broadcast_to(v,full)
    S=[load(g) for g in range(16)]
    X=[jnp.where(lane==sub+8*g,1.0,0.0).astype(jnp.float32) for g in range(16)]
    for g in range(16):
        V=S[g]; XV=X[g]
        col=[bc(V[:,8*g+j:8*g+j+1]) for j in range(8)]
        a={(i,j):bc(col[j][i:i+1,:]) for j in range(8) for i in range(j,8)}
        y=[bc(V[i:i+1,:]) for i in range(8)]
        w=[bc(XV[i:i+1,:]) for i in range(8)]
        r=[None]*8; m={}
        XI=jnp.zeros(full,jnp.float32)
        for j in range(8):
            rs=lax.rsqrt(a[j,j]); r[j]=rs*rs
            XI=jnp.where(sub==j,w[j]*rs,XI)
            for i in range(j+1,8):
                m[i,j]=a[i,j]*r[j]
            for k in range(j+1,8):
                for i in range(k,8):
                    a[i,k]=a[i,k]-m[i,j]*a[k,j]
            for i in range(j+1,8):
                y[i]=y[i]-m[i,j]*y[j]
                w[i]=w[i]-m[i,j]*w[j]
        store_l(g,XI)
        if g==7:
            poll()
        if g<15:
            z=[None]*8; zx=[None]*8
            for j in range(7,-1,-1):
                z[j]=y[j]*r[j]; zx[j]=w[j]*r[j]
                for k in range(7,j,-1):
                    z[j]=z[j]-m[k,j]*z[k]; zx[j]=zx[j]-m[k,j]*zx[k]
            for h in range(g+1,16):
                s=S[h]; x=X[h]
                cb=[bc(s[:,8*g+j:8*g+j+1]) for j in range(8)]
                t=[cb[j]*z[j] for j in range(8)]
                tx=[cb[j]*zx[j] for j in range(8)]
                tree=lambda t:((t[0]+t[1])+(t[2]+t[3]))+((t[4]+t[5])+(t[6]+t[7]))
                S[h]=s-tree(t); X[h]=x-tree(tx)

MESH = pl.DeviceIdType.MESH
CORNER = ((0, 0), (1, 0), (1, 1), (2, 0), (2, 1), (2, 2))
PIECES = 48


def comm_kernel(mat, A, B, V, a0, C, W, M, tile, dref, lref, l0, m0, asend, arecv, ysend, crecv, csend, psend, precv, brecv, bsend, loc):
    p = lax.axis_index("row")
    q = lax.axis_index("col")
    x = p // 8
    z = p % 8
    core = q % 2
    partner = q + 1 - 2 * core

    def at(px, pz):
        return (lax.rem(px + 4, 4) * 8 + lax.rem(pz + 8, 8), q)

    def along(d):
        return (p, lax.rem(q + d, 8))

    def rcopy(src, dst, ss, rs, dev):
        return pltpu.make_async_remote_copy(
            src_ref=src, dst_ref=dst, send_sem=ss, recv_sem=rs, device_id=dev, device_id_type=MESH
        )

    def arrived(ref, sem):
        pltpu.make_async_copy(ref, ref, sem).wait()

    for a in range(2):
        pltpu.make_async_copy(mat.at[a, 0, :, 0, 0, :], a0.at[a], loc.at[4 + a]).start()

    barrier = pltpu.get_barrier_semaphore()
    for d in range(1, 8):
        pl.semaphore_signal(barrier, inc=1, device_id=along(d), device_id_type=MESH)
    for dx, dz in ((1, 0), (-1, 0), (0, 1), (0, -1)):
        pl.semaphore_signal(barrier, inc=1, device_id=at(x + dx, z + dz), device_id_type=MESH)
    pl.semaphore_wait(barrier, 11)
    for a in range(2):
        arrived(a0.at[a], loc.at[4 + a])

    def quarter(c, u):
        return pl.ds(pl.multiple_of((c + 2 * u) * 64, 64), 64)

    def ycopy(idx, d, u):
        rows = quarter(lax.rem(q + d, 2), u)
        return rcopy(a0.at[0, rows, :], C.at[idx, rows, :], ysend.at[(d - 1) * 2 + u], crecv.at[idx, u], along(d))

    for idx, (i, j) in enumerate(CORNER):

        @pl.when((p == i) & (q == j))
        def _(idx=idx):
            pltpu.make_async_copy(a0.at[0], C.at[idx], loc.at[2]).start()
            for u in range(2):
                for d in range(1, 8):
                    ycopy(idx, d, u).start()
            pltpu.make_async_copy(a0.at[0], C.at[idx], loc.at[2]).wait()

    first = lax.rem(z - q + 8, 8)

    def acopy(k, a, d):
        return rcopy(a0.at[a], A.at[k, a], asend.at[a, d - 1], arecv.at[k, a], along(d))

    for k in range(3):

        @pl.when(q == k)
        def _(k=k):
            for a in range(2):
                pltpu.make_async_copy(a0.at[a], A.at[k, a], loc.at[a]).start()
            for now in (True, False):
                for a in range(2):
                    for d in range(1, 8):

                        @pl.when((d == first) if now else (d != first))
                        def _(a=a, d=d):
                            acopy(k, a, d).start()

    def hops(x0, z0, typ, sx, sz):
        dx = lax.rem(x - x0 + 4, 4)
        dz = lax.rem(sz * (z - z0) + 16, 8)
        cz = (typ == 1) | (dx == 0)
        cx = (typ == 0) | (dz == 0)
        return (
            ((x, z + sz), cz & (dz <= 3)),
            ((x, z - sz), cz & ((dz == 0) | (dz >= 6))),
            ((x + 1, z), cx & ((dx == 0) | ((dx == 1) & (sx == 1)))),
            ((x - 1, z), cx & ((dx == 0) | ((dx == 3) & (sx == 0)))),
        )

    def corner(e, end):
        idx, u = e // 2, e % 2
        i, j = CORNER[idx]
        ref = C.at[idx, quarter(core, u), :]
        other = C.at[idx, quarter(1 - core, u), :]
        mine = (p == i) & (q == j)
        its = (p == i) & (partner == j)
        if end is False:

            @pl.when(jnp.logical_not(mine))
            def _():
                arrived(ref, crecv.at[idx, u])

        if end is not None:

            for n, (dev, cond) in enumerate(hops(0, i, u, idx % 2, 1)):

                @pl.when(cond)
                def _(n=n, dev=dev):
                    c = rcopy(ref, ref, csend.at[e, n], crecv.at[idx, u], at(*dev))
                    c.wait_send() if end else c.start()

            @pl.when(jnp.logical_not(its))
            def _():
                c = rcopy(ref, ref, psend.at[e], precv.at[e], (p, partner))
                c.wait_send() if end else c.start()

        if end is None:

            @pl.when(jnp.logical_not(mine))
            def _():
                arrived(other, precv.at[e])

    dz = lax.rem(z - q + 8, 8)
    root = dz == 0

    def half(x0, r):
        h = r % 2
        a = (r // 2) % 2
        k = r // 4
        return B.at[x0, a, k, pl.ds(pl.multiple_of(h * 128, 128), 128), :]

    def send(x0, r, n, dev, cond, end):
        e = x0 * 12 + r

        @pl.when(cond)
        def _():
            c = rcopy(half(x0, r), half(x0, r), bsend.at[e, n], brecv.at[e], at(*dev))
            c.wait_send() if end else c.start()

    def own(r, end):
        a = (r // 2) % 2
        k = r // 4
        if not end:

            @pl.when(root & (r % 2 == 0))
            def _():
                @pl.when(q == k)
                def _():
                    arrived(A.at[k, a], loc.at[a])

                @pl.when(q != k)
                def _():
                    arrived(A.at[k, a], arecv.at[k, a])

                c = pltpu.make_async_copy(A.at[k, a], B.at[x, a, k], loc.at[3])
                c.start()
                c.wait()

            @pl.when(jnp.logical_not(root))
            def _():
                arrived(half(x, r), brecv.at[x * 12 + r])

        send(x, r, 0, (x, z + 1), dz <= 3, end)
        send(x, r, 1, (x, z - 1), root | (dz >= 6), end)
        send(x, r, 2, (x + 1, z), p >= 0, end)
        send(x, r, 3, (x - 1, z), p >= 0, end)

    left = lax.rem(x + 3, 4)
    right = lax.rem(x + 1, 4)
    across = lax.rem(x + 2, 4)

    def passing(r, end):
        if not end:
            arrived(half(left, r), brecv.at[left * 12 + r])
        send(left, r, 0, (x + 1, z), r % 2 == 0, end)
        if not end:
            arrived(half(right, r), brecv.at[right * 12 + r])
        send(right, r, 1, (x - 1, z), r % 2 == 1, end)


    def go(r, _):
        @pl.when(r < 12)
        def _():
            own(r, False)

        @pl.when(r > 0)
        def _():
            passing(r - 1, False)

        return 0


    for e in range(12):
        corner(e, False)
        if e % 3 == 2:
            go(e // 3, 0)
    for e in range(12):
        corner(e, None)

    tile[...] = C[0]
    dref[...] = tile[:128, :128]

    def step(t, _):
        def poll(r):
            @pl.when(r < 13)
            def _():
                go(r, 0)

        def load(g):
            return dref[8 * g : 8 * g + 8, :]

        def store(g, v):
            lref[8 * g : 8 * g + 8, :] = v

        poll(4 + 2 * t)
        factor128(load, store, lambda: poll(5 + 2 * t))

        @pl.when(t % 2 == 0)
        def _():
            li = lref[...]
            m = tdot(tile[128:, :128], li)
            l0[...] = li
            m0[...] = m
            dref[...] = tile[128:, 128:] - tdot(m, m)

        for k in range(3):

            @pl.when(t == 2 * k + 1)
            def _(k=k):
                o = 256 * k
                li = lref[...]
                V[o : o + 128, o : o + 128] = l0[...]
                V[o : o + 128, o + 128 : o + 256] = jnp.zeros((128, 128), jnp.float32)
                V[o + 128 : o + 256, o + 128 : o + 256] = li
                V[o + 128 : o + 256, o : o + 128] = -ndot(li, ndot(m0[...], l0[...]))
                v = V[o : o + 256, o : o + 256]
                if k == 0:
                    m1 = tdot(C[1], v)
                    m2 = tdot(C[3], v)
                    tile[...] = C[2] - tdot(m1, m1)
                    dref[...] = tile[:128, :128]
                    W[0] = C[4] - tdot(m2, m1)
                    W[1] = C[5] - tdot(m2, m2)
                    M[0] = ndot(m1, v)
                    M[1] = ndot(m2, v)
                if k == 1:
                    m = tdot(W[0], v)
                    tile[...] = W[1] - tdot(m, m)
                    dref[...] = tile[:128, :128]
                    V[256:512, :256] = -ndot(v, M[0])
                    M[1] += ndot(m, V[256:512, :256])
                    M[0] = ndot(m, v)
                if k == 2:
                    V[512:, :256] = -ndot(v, M[1])
                    V[512:, 256:512] = -ndot(v, M[0])

        return 0

    lax.fori_loop(0, 6, step, 0)

    def last(r, _):
        arrived(half(across, r), brecv.at[across * 12 + r])
        return 0

    lax.fori_loop(0, 12, last, 0)

    for k in range(3):
        for a in range(2):

            @pl.when((z != q) & (q == k))
            def _(k=k, a=a):
                arrived(A.at[k, a], loc.at[a])

            @pl.when((z != q) & (q != k))
            def _(k=k, a=a):
                arrived(A.at[k, a], arecv.at[k, a])

    for e in range(12):
        corner(e, True)

    def done(r, _):
        own(r, True)
        passing(r, True)
        return 0

    lax.fori_loop(0, 12, done, 0)

    for idx, (i, j) in enumerate(CORNER):

        @pl.when((p == i) & (q == j))
        def _(idx=idx):
            for d in range(1, 8):
                for u in range(2):
                    ycopy(idx, d, u).wait_send()

    for k in range(3):

        @pl.when(q == k)
        def _(k=k):
            for a in range(2):
                for d in range(1, 8):
                    acopy(k, a, d).wait_send()


def gather(matrix):
    f32 = jnp.float32
    dma = pltpu.SemaphoreType.DMA
    vm = pltpu.VMEM
    return pl.pallas_call(
        comm_kernel,
        out_shape=(
            jax.ShapeDtypeStruct((3, 2, 256, 256), f32),
            jax.ShapeDtypeStruct((4, 2, 3, 256, 256), f32),
            jax.ShapeDtypeStruct((768, 768), f32),
        ),
        in_specs=[pl.BlockSpec(memory_space=pl.ANY)],
        out_specs=(pl.BlockSpec(memory_space=vm),) * 3,
        scratch_shapes=[
            vm((2, 256, 256), f32), vm((6, 256, 256), f32), vm((2, 256, 256), f32), vm((2, 256, 256), f32),
            vm((256, 256), f32), vm((128, 128), f32), vm((128, 128), f32), vm((128, 128), f32), vm((128, 128), f32),
            dma((2, 7)), dma((3, 2)), dma((14,)), dma((6, 2)), dma((12, 4)), dma((12,)), dma((12,)),
            dma((PIECES,)), dma((PIECES, 4)), dma((6,)),
        ],
        compiler_params=pltpu.CompilerParams(collective_id=0, has_side_effects=True, vmem_limit_bytes=44 << 20),
    )(matrix)


def split(v):
    hi = v.astype(jnp.bfloat16)
    return hi, (v - hi.astype(jnp.float32)).astype(jnp.bfloat16)


def update_kernel(mat, A, B, V, out, panel, vh, vl, ph, plo):
    c = pl.program_id(0)
    p = lax.axis_index("row")
    q = lax.axis_index("col")

    def bdot(a, b):
        return lax.dot_general(a, b, (((1,), (1,)), ((), ())), preferred_element_type=jnp.float32)

    def rows(load, number, put):
        parts = [split(load(m)) for m in range(3)]
        for n in range(3):
            total = None
            for m in range(n + 1):
                h, l = parts[m]
                at = (slice(256 * n, 256 * n + 256), slice(256 * m, 256 * m + 256))
                term = bdot(h, vh[at]) + (bdot(h, vl[at]) + bdot(l, vh[at]))
                total = term if total is None else total + term
            put(n, jnp.where(number >= n, total, 0.0))

    @pl.when(c == 0)
    def _():
        for n in range(3):
            at = (slice(256 * n, 256 * n + 256), slice(0, 256 * n + 256))
            vh[at], vl[at] = split(V[at])
        for a in range(2):

            def put(n, value):
                panel[a, 0, :, 256 * n : 256 * n + 256] = value
                ph[a, :, 256 * n : 256 * n + 256], plo[a, :, 256 * n : 256 * n + 256] = split(value)

            rows(lambda m: A[m, a], a * 32 + p, put)

    mirrored = [None] * 3

    def keep(n, value):
        mirrored[n] = split(value)

    rows(lambda m: B[0, 0, m], c * 8 + q, keep)
    mh = jnp.concatenate([m[0] for m in mirrored], axis=1)
    ml = jnp.concatenate([m[1] for m in mirrored], axis=1)
    for a in range(2):
        term = bdot(ph[a], mh) + (bdot(ph[a], ml) + bdot(plo[a], mh))
        out[a, 0, :, 0, 0, :] = mat[a, 0, :, 0, 0, :] - term


def update(matrix, A, B, V):
    f32 = jnp.float32
    bf16 = jnp.bfloat16
    vm = pltpu.VMEM
    block = pl.BlockSpec((2, 1, 256, 1, 1, 256), lambda c: (0, 0, 0, c, 0, 0))
    return pl.pallas_call(
        update_kernel,
        grid=(8,),
        out_shape=(jax.ShapeDtypeStruct(matrix.shape, f32), jax.ShapeDtypeStruct((2, 1, 256, 768), f32)),
        in_specs=[
            block,
            pl.BlockSpec((3, 2, 256, 256), lambda c: (0, 0, 0, 0)),
            pl.BlockSpec((1, 1, 3, 256, 256), lambda c: (c % 4, c // 4, 0, 0, 0)),
            pl.BlockSpec((768, 768), lambda c: (0, 0)),
        ],
        out_specs=(block, pl.BlockSpec((2, 1, 256, 768), lambda c: (0, 0, 0, 0))),
        scratch_shapes=[vm((768, 768), bf16), vm((768, 768), bf16), vm((2, 256, 768), bf16), vm((2, 256, 768), bf16)],
        compiler_params=pltpu.CompilerParams(vmem_limit_bytes=44 << 20),
    )(matrix, A, B, V)


def body(matrix):
    A, B, V = gather(matrix)
    return update(matrix, A, B, V)


def solution(mesh):
    in_specs = (P(None, "row", None, None, "col", None),)
    out_specs = (P(None, "row", None, None, "col", None), P(None, "row", None, None))
    return jax.shard_map(body, mesh=mesh, in_specs=in_specs, out_specs=out_specs, check_vma=False)
```

```python
import jax
import jax.numpy as jnp
from jax import lax
from jax.experimental import pallas as pl
from jax.experimental.pallas import tpu as pltpu
from jax.sharding import PartitionSpec as P

HI = lax.Precision.HIGHEST


def dots(a, b, dim, precision=HI):
    return lax.dot_general(a, b, (((1,), (dim,)), ((), ())), precision=precision, preferred_element_type=jnp.float32)


def tdot(a, b):
    return dots(a, b, 1)


def ndot(a, b):
    return dots(a, b, 0)


def factor128(load, store_l, poll):
    sub = lax.broadcasted_iota(jnp.int32,(8,128),0)
    lane = lax.broadcasted_iota(jnp.int32,(8,128),1)
    full=(8,128)
    bc=lambda v: jnp.broadcast_to(v,full)
    S=[load(g) for g in range(16)]
    X=[jnp.where(lane==sub+8*g,1.0,0.0).astype(jnp.float32) for g in range(16)]
    for g in range(16):
        V=S[g]; XV=X[g]
        col=[bc(V[:,8*g+j:8*g+j+1]) for j in range(8)]
        a={(i,j):bc(col[j][i:i+1,:]) for j in range(8) for i in range(j,8)}
        y=[bc(V[i:i+1,:]) for i in range(8)]
        w=[bc(XV[i:i+1,:]) for i in range(8)]
        r=[None]*8; m={}
        XI=jnp.zeros(full,jnp.float32)
        for j in range(8):
            rs=lax.rsqrt(a[j,j]); r[j]=rs*rs
            XI=jnp.where(sub==j,w[j]*rs,XI)
            for i in range(j+1,8):
                m[i,j]=a[i,j]*r[j]
            for k in range(j+1,8):
                for i in range(k,8):
                    a[i,k]=a[i,k]-m[i,j]*a[k,j]
            for i in range(j+1,8):
                y[i]=y[i]-m[i,j]*y[j]
                w[i]=w[i]-m[i,j]*w[j]
        store_l(g,XI)
        if g in POLLS:
            poll(POLLS.index(g))
        if g<15:
            z=[None]*8; zx=[None]*8
            for j in range(7,-1,-1):
                z[j]=y[j]*r[j]; zx[j]=w[j]*r[j]
                for k in range(7,j,-1):
                    z[j]=z[j]-m[k,j]*z[k]; zx[j]=zx[j]-m[k,j]*zx[k]
            for h in range(g+1,16):
                s=S[h]; x=X[h]
                cb=[bc(s[:,8*g+j:8*g+j+1]) for j in range(8)]
                t=[cb[j]*z[j] for j in range(8)]
                tx=[cb[j]*zx[j] for j in range(8)]
                tree=lambda t:((t[0]+t[1])+(t[2]+t[3]))+((t[4]+t[5])+(t[6]+t[7]))
                S[h]=s-tree(t); X[h]=x-tree(tx)

MESH = pl.DeviceIdType.MESH
CORNER = ((0, 0), (1, 0), (1, 1), (2, 0), (2, 1), (2, 2))
POLLS = (5, 10)
PIECES = 48


def comm_kernel(mat, A, B, V, a0, C, W, M, tile, dref, lref, l0, m0, asend, arecv, ysend, crecv, csend, psend, precv, brecv, bsend, fsend, loc):
    p = lax.axis_index("row")
    q = lax.axis_index("col")
    x = p // 8
    z = p % 8
    core = q % 2
    partner = q + 1 - 2 * core

    def at(px, pz):
        return (lax.rem(px + 4, 4) * 8 + lax.rem(pz + 8, 8), q)

    def along(d):
        return (p, lax.rem(q + d, 8))

    def rcopy(src, dst, ss, rs, dev):
        return pltpu.make_async_remote_copy(
            src_ref=src, dst_ref=dst, send_sem=ss, recv_sem=rs, device_id=dev, device_id_type=MESH
        )

    def arrived(ref, sem):
        pltpu.make_async_copy(ref, ref, sem).wait()

    for a in range(2):
        pltpu.make_async_copy(mat.at[a, 0, :, 0, 0, :], a0.at[a], loc.at[4 + a]).start()

    barrier = pltpu.get_barrier_semaphore()
    for d in range(1, 8):
        pl.semaphore_signal(barrier, inc=1, device_id=along(d), device_id_type=MESH)
    for dx, dz in ((1, 0), (-1, 0), (0, 1), (0, -1)):
        pl.semaphore_signal(barrier, inc=1, device_id=at(x + dx, z + dz), device_id_type=MESH)
    pl.semaphore_wait(barrier, 11)
    for a in range(2):
        arrived(a0.at[a], loc.at[4 + a])

    def quarter(c, u):
        return pl.ds(pl.multiple_of((c + 2 * u) * 64, 64), 64)

    def ycopy(idx, d, u):
        rows = quarter(lax.rem(q + d, 2), u)
        return rcopy(a0.at[0, rows, :], C.at[idx, rows, :], ysend.at[(d - 1) * 2 + u], crecv.at[idx, u], along(d))

    for idx, (i, j) in enumerate(CORNER):

        @pl.when((p == i) & (q == j))
        def _(idx=idx):
            pltpu.make_async_copy(a0.at[0], C.at[idx], loc.at[2]).start()
            for u in range(2):
                for d in range(1, 8):
                    ycopy(idx, d, u).start()
            pltpu.make_async_copy(a0.at[0], C.at[idx], loc.at[2]).wait()

    first = lax.rem(z - q + 8, 8)

    def acopy(k, a, d):
        return rcopy(a0.at[a], A.at[k, a], asend.at[a, d - 1], arecv.at[k, a], along(d))

    def direct(a, d):
        to = lax.rem(q + d, 8)
        return (to // 2 == q // 2) | (to % 2 == a)

    def forward(k, end):
        ref = A.at[k, core]

        @pl.when(q // 2 != k // 2)
        def _():
            if not end:

                @pl.when(z != q)
                def _():
                    arrived(ref, arecv.at[k, core])

            @pl.when(partner != z)
            def _():
                c = rcopy(ref, ref, fsend.at[k], arecv.at[k, core], (p, partner))
                c.wait_send() if end else c.start()

    for k in range(3):

        @pl.when(q == k)
        def _(k=k):
            for a in range(2):
                pltpu.make_async_copy(a0.at[a], A.at[k, a], loc.at[a]).start()
                for d in range(1, 8):

                    @pl.when(d == first)
                    def _(a=a, d=d):
                        acopy(k, a, d).start()

    def hops(x0, z0, typ, sx, sz):
        dx = lax.rem(x - x0 + 4, 4)
        dz = lax.rem(sz * (z - z0) + 16, 8)
        cz = (typ == 1) | (dx == 0)
        cx = (typ == 0) | (dz == 0)
        return (
            ((x, z + sz), cz & (dz <= 3)),
            ((x, z - sz), cz & ((dz == 0) | (dz >= 6))),
            ((x + 1, z), cx & ((dx == 0) | ((dx == 1) & (sx == 1)))),
            ((x - 1, z), cx & ((dx == 0) | ((dx == 3) & (sx == 0)))),
        )

    def corner(e, end):
        idx, u = e // 2, e % 2
        i, j = CORNER[idx]
        ref = C.at[idx, quarter(core, u), :]
        other = C.at[idx, quarter(1 - core, u), :]
        mine = (p == i) & (q == j)
        its = (p == i) & (partner == j)
        if end is False:

            @pl.when(jnp.logical_not(mine))
            def _():
                arrived(ref, crecv.at[idx, u])

        if end is not None:

            for n, (dev, cond) in enumerate(hops(0, i, u, idx % 2, 1)):

                @pl.when(cond)
                def _(n=n, dev=dev):
                    c = rcopy(ref, ref, csend.at[e, n], crecv.at[idx, u], at(*dev))
                    c.wait_send() if end else c.start()

            @pl.when(jnp.logical_not(its))
            def _():
                c = rcopy(ref, ref, psend.at[e], precv.at[e], (p, partner))
                c.wait_send() if end else c.start()

        if end is None:

            @pl.when(jnp.logical_not(mine))
            def _():
                arrived(other, precv.at[e])

    dz = lax.rem(z - q + 8, 8)
    root = dz == 0

    def half(x0, r):
        h = r % 2
        a = (r // 2) % 2
        k = r // 4
        return B.at[x0, a, k, pl.ds(pl.multiple_of(h * 128, 128), 128), :]

    def send(x0, r, n, dev, cond, end):
        e = x0 * 12 + r

        @pl.when(cond)
        def _():
            c = rcopy(half(x0, r), half(x0, r), bsend.at[e, n], brecv.at[e], at(*dev))
            c.wait_send() if end else c.start()

    def emit(r, who, end):
        send(x, r, 0, (x, z + 1), who & (dz <= 3), end)
        send(x, r, 1, (x, z - 1), who & (root | (dz >= 6)), end)
        send(x, r, 2, (x + 1, z), who, end)
        send(x, r, 3, (x - 1, z), who, end)

    def lead(r):
        a = (r // 2) % 2
        k = r // 4

        @pl.when(root & (r % 2 == 0))
        def _():
            @pl.when(q == k)
            def _():
                arrived(A.at[k, a], loc.at[a])

            @pl.when(q != k)
            def _():
                arrived(A.at[k, a], arecv.at[k, a])

            c = pltpu.make_async_copy(A.at[k, a], B.at[x, a, k], loc.at[3])
            c.start()
            c.wait()

        emit(r, root, False)

    def own(r):
        @pl.when(jnp.logical_not(root))
        def _():
            arrived(half(x, r), brecv.at[x * 12 + r])

        emit(r, jnp.logical_not(root), False)

    left = lax.rem(x + 3, 4)
    right = lax.rem(x + 1, 4)
    across = lax.rem(x + 2, 4)

    def passing(r, end):
        if not end:
            arrived(half(left, r), brecv.at[left * 12 + r])
        send(left, r, 0, (x + 1, z), r % 2 == 0, end)
        if not end:
            arrived(half(right, r), brecv.at[right * 12 + r])
        send(right, r, 1, (x - 1, z), r % 2 == 1, end)


    def go(r, _):
        @pl.when(r + 3 < 12)
        def _():
            lead(r + 3)

        @pl.when(r < 12)
        def _():
            own(r)

        @pl.when(r > 0)
        def _():
            passing(r - 1, False)

        return 0


    for e in range(12):
        corner(e, False)
        for r, after in enumerate((3, 7, 11)):
            if e == after:
                lead(r)
    for e in range(12):
        corner(e, None)

    late = jnp.minimum(dz, 8 - dz)
    tile[...] = C[0]
    dref[...] = tile[:128, :128]

    def step(t, _):
        def poll(r):
            @pl.when((r >= 0) & (r < 13))
            def _():
                go(r, 0)

        for k in range(3):
            for a in range(2):

                @pl.when((q == k) & (t == 0))
                def _(k=k, a=a):
                    for d in range(1, 8):

                        @pl.when((d != first) & direct(a, d))
                        def _(d=d):
                            acopy(k, a, d).start()

        @pl.when(t == 4)
        def _():
            for k in range(3):
                forward(k, False)

        def load(g):
            return dref[8 * g : 8 * g + 8, :]

        def store(g, v):
            lref[8 * g : 8 * g + 8, :] = v

        poll(3 * t - late)
        factor128(load, store, lambda i: poll(1 + 3 * t + i - late))

        @pl.when(t % 2 == 0)
        def _():
            li = lref[...]
            m = tdot(tile[128:, :128], li)
            l0[...] = li
            m0[...] = m
            dref[...] = tile[128:, 128:] - tdot(m, m)

        for k in range(3):

            @pl.when(t == 2 * k + 1)
            def _(k=k):
                o = 256 * k
                li = lref[...]
                V[o : o + 128, o : o + 128] = l0[...]
                V[o : o + 128, o + 128 : o + 256] = jnp.zeros((128, 128), jnp.float32)
                V[o + 128 : o + 256, o + 128 : o + 256] = li
                V[o + 128 : o + 256, o : o + 128] = -ndot(li, ndot(m0[...], l0[...]))
                v = V[o : o + 256, o : o + 256]
                if k == 0:
                    m1 = tdot(C[1], v)
                    m2 = tdot(C[3], v)
                    tile[...] = C[2] - tdot(m1, m1)
                    dref[...] = tile[:128, :128]
                    W[0] = C[4] - tdot(m2, m1)
                    W[1] = C[5] - tdot(m2, m2)
                    M[0] = ndot(m1, v)
                    M[1] = ndot(m2, v)
                if k == 1:
                    m = tdot(W[0], v)
                    tile[...] = W[1] - tdot(m, m)
                    dref[...] = tile[:128, :128]
                    V[256:512, :256] = -ndot(v, M[0])
                    M[1] += ndot(m, V[256:512, :256])
                    M[0] = ndot(m, v)
                if k == 2:
                    V[512:, :256] = -ndot(v, M[1])
                    V[512:, 256:512] = -ndot(v, M[0])

        return 0

    lax.fori_loop(0, 6, step, 0)
    lax.fori_loop(jnp.minimum(18 - late, 13), 13, go, 0)

    def last(r, _):
        arrived(half(across, r), brecv.at[across * 12 + r])
        return 0

    lax.fori_loop(0, 12, last, 0)

    for k in range(3):
        for a in range(2):

            @pl.when((z != q) & (q == k))
            def _(k=k, a=a):
                arrived(A.at[k, a], loc.at[a])

            @pl.when((z != q) & (q != k) & ((q // 2 == k // 2) | (core != a)))
            def _(k=k, a=a):
                arrived(A.at[k, a], arecv.at[k, a])

    for e in range(12):
        corner(e, True)

    def done(r, _):
        emit(r, p >= 0, True)
        passing(r, True)
        return 0

    lax.fori_loop(0, 12, done, 0)

    for idx, (i, j) in enumerate(CORNER):

        @pl.when((p == i) & (q == j))
        def _(idx=idx):
            for d in range(1, 8):
                for u in range(2):
                    ycopy(idx, d, u).wait_send()

    for k in range(3):

        @pl.when(q == k)
        def _(k=k):
            for a in range(2):
                for d in range(1, 8):

                    @pl.when((d == first) | direct(a, d))
                    def _(a=a, d=d):
                        acopy(k, a, d).wait_send()

    for k in range(3):
        forward(k, True)


def gather(matrix):
    f32 = jnp.float32
    dma = pltpu.SemaphoreType.DMA
    vm = pltpu.VMEM
    return pl.pallas_call(
        comm_kernel,
        out_shape=(
            jax.ShapeDtypeStruct((3, 2, 256, 256), f32),
            jax.ShapeDtypeStruct((4, 2, 3, 256, 256), f32),
            jax.ShapeDtypeStruct((768, 768), f32),
        ),
        in_specs=[pl.BlockSpec(memory_space=pl.ANY)],
        out_specs=(pl.BlockSpec(memory_space=vm),) * 3,
        scratch_shapes=[
            vm((2, 256, 256), f32), vm((6, 256, 256), f32), vm((2, 256, 256), f32), vm((2, 256, 256), f32),
            vm((256, 256), f32), vm((128, 128), f32), vm((128, 128), f32), vm((128, 128), f32), vm((128, 128), f32),
            dma((2, 7)), dma((3, 2)), dma((14,)), dma((6, 2)), dma((12, 4)), dma((12,)), dma((12,)),
            dma((PIECES,)), dma((PIECES, 4)), dma((3,)), dma((6,)),
        ],
        compiler_params=pltpu.CompilerParams(collective_id=0, has_side_effects=True, vmem_limit_bytes=44 << 20),
    )(matrix)


def split(v):
    hi = v.astype(jnp.bfloat16)
    return hi, (v - hi.astype(jnp.float32)).astype(jnp.bfloat16)


def update_kernel(mat, A, B, V, out, panel, vh, vl, ph, plo):
    c = pl.program_id(0)
    p = lax.axis_index("row")
    q = lax.axis_index("col")

    def bdot(a, b):
        return lax.dot_general(a, b, (((1,), (1,)), ((), ())), preferred_element_type=jnp.float32)

    def rows(load, number, put):
        parts = [split(load(m)) for m in range(3)]
        for n in range(3):
            total = None
            for m in range(n + 1):
                h, l = parts[m]
                at = (slice(256 * n, 256 * n + 256), slice(256 * m, 256 * m + 256))
                term = bdot(h, vh[at]) + (bdot(h, vl[at]) + bdot(l, vh[at]))
                total = term if total is None else total + term
            put(n, jnp.where(number >= n, total, 0.0))

    @pl.when(c == 0)
    def _():
        for n in range(3):
            at = (slice(256 * n, 256 * n + 256), slice(0, 256 * n + 256))
            vh[at], vl[at] = split(V[at])
        for a in range(2):

            def put(n, value):
                panel[a, 0, :, 256 * n : 256 * n + 256] = value
                ph[a, :, 256 * n : 256 * n + 256], plo[a, :, 256 * n : 256 * n + 256] = split(value)

            rows(lambda m: A[m, a], a * 32 + p, put)

    mirrored = [None] * 3

    def keep(n, value):
        mirrored[n] = split(value)

    rows(lambda m: B[0, 0, m], c * 8 + q, keep)
    mh = jnp.concatenate([m[0] for m in mirrored], axis=1)
    ml = jnp.concatenate([m[1] for m in mirrored], axis=1)
    for a in range(2):
        term = bdot(ph[a], mh) + (bdot(ph[a], ml) + bdot(plo[a], mh))
        out[a, 0, :, 0, 0, :] = mat[a, 0, :, 0, 0, :] - term


def update(matrix, A, B, V):
    f32 = jnp.float32
    bf16 = jnp.bfloat16
    vm = pltpu.VMEM
    block = pl.BlockSpec((2, 1, 256, 1, 1, 256), lambda c: (0, 0, 0, c, 0, 0))
    return pl.pallas_call(
        update_kernel,
        grid=(8,),
        out_shape=(jax.ShapeDtypeStruct(matrix.shape, f32), jax.ShapeDtypeStruct((2, 1, 256, 768), f32)),
        in_specs=[
            block,
            pl.BlockSpec((3, 2, 256, 256), lambda c: (0, 0, 0, 0)),
            pl.BlockSpec((1, 1, 3, 256, 256), lambda c: (c % 4, c // 4, 0, 0, 0)),
            pl.BlockSpec((768, 768), lambda c: (0, 0)),
        ],
        out_specs=(block, pl.BlockSpec((2, 1, 256, 768), lambda c: (0, 0, 0, 0))),
        scratch_shapes=[vm((768, 768), bf16), vm((768, 768), bf16), vm((2, 256, 768), bf16), vm((2, 256, 768), bf16)],
        compiler_params=pltpu.CompilerParams(vmem_limit_bytes=44 << 20),
    )(matrix, A, B, V)


def body(matrix):
    A, B, V = gather(matrix)
    return update(matrix, A, B, V)


def solution(mesh):
    in_specs = (P(None, "row", None, None, "col", None),)
    out_specs = (P(None, "row", None, None, "col", None), P(None, "row", None, None))
    return jax.shard_map(body, mesh=mesh, in_specs=in_specs, out_specs=out_specs, check_vma=False)
```
